32 devices in a mesh: row: 4 (over y, x), col: 8 (over z, core).
Axes of the slice: x: 2, y: 2, z: 4, core: 2. Of those that a mesh axis runs over, the one named last changes fastest.
Arguments:
- tubes: bfloat16 [64, 1568, 1536], P(('row', 'col')), may hold values from -6 to 6
- tube_order: int32 [64, 1568], P(('row', 'col')), may hold values from 0 to 1567, each once within a row
- step_count: int32 [1], replicated, may hold values from 2 to 20
- embed_weight: float32 [1536, 768], P('row', 'col'), may hold values from -0.15625 to 0.15625
- embed_first: float32 [1536, 768], P('row', 'col'), may hold values from -9.1552734e-05 to 9.1552734e-05
- embed_second: float32 [1536, 768], P('row', 'col'), may hold values from 2.1121419e-11 to 3.379427e-10
- encoder_wide_weight: float32 [2, 768, 6144], P(None, 'row', 'col'), may hold values from -0.21875 to 0.21875
- encoder_wide_first: float32 [2, 768, 6144], P(None, 'row', 'col'), may hold values from -9.1552734e-05 to 9.1552734e-05
- encoder_wide_second: float32 [2, 768, 6144], P(None, 'row', 'col'), may hold values from 2.1121419e-11 to 3.379427e-10
- encoder_down_weight: float32 [2, 3072, 768], P(None, 'row', 'col'), may hold values from -0.109375 to 0.109375
- encoder_down_first: float32 [2, 3072, 768], P(None, 'row', 'col'), may hold values from -9.1552734e-05 to 9.1552734e-05
- encoder_down_second: float32 [2, 3072, 768], P(None, 'row', 'col'), may hold values from 2.1121419e-11 to 3.379427e-10
- decoder_wide_weight: float32 [384, 3072], P('row', 'col'), may hold values from -0.3125 to 0.3125
- decoder_wide_first: float32 [384, 3072], P('row', 'col'), may hold values from -9.1552734e-05 to 9.1552734e-05
- decoder_wide_second: float32 [384, 3072], P('row', 'col'), may hold values from 2.1121419e-11 to 3.379427e-10
- decoder_rows_weight: float32 [2304, 384], P('row', 'col'), may hold values from -0.15625 to 0.15625
- decoder_rows_first: float32 [2304, 384], P('row', 'col'), may hold values from -9.1552734e-05 to 9.1552734e-05
- decoder_rows_second: float32 [2304, 384], P('row', 'col'), may hold values from 2.1121419e-11 to 3.379427e-10
- pixel_head_weight: float32 [384, 1536], replicated, may hold values from -0.3125 to 0.3125
- pixel_head_first: float32 [384, 1536], replicated, may hold values from -9.1552734e-05 to 9.1552734e-05
- pixel_head_second: float32 [384, 1536], replicated, may hold values from 2.1121419e-11 to 3.379427e-10
- vectors_weight: float32 [5376], replicated, may hold values from 0.5 to 1.5
- vectors_first: float32 [5376], replicated, may hold values from -9.1552734e-05 to 9.1552734e-05
- vectors_second: float32 [5376], replicated, may hold values from 2.1121419e-11 to 3.379427e-10
Outputs:
- loss: float32 [], replicated
- new_embed_weight: float32 [1536, 768], P('row', 'col')
- new_embed_first: float32 [1536, 768], P('row', 'col')
- new_embed_second: float32 [1536, 768], P('row', 'col')
- new_encoder_wide_weight: float32 [2, 768, 6144], P(None, 'row', 'col')
- new_encoder_wide_first: float32 [2, 768, 6144], P(None, 'row', 'col')
- new_encoder_wide_second: float32 [2, 768, 6144], P(None, 'row', 'col')
- new_encoder_down_weight: float32 [2, 3072, 768], P(None, 'row', 'col')
- new_encoder_down_first: float32 [2, 3072, 768], P(None, 'row', 'col')
- new_encoder_down_second: float32 [2, 3072, 768], P(None, 'row', 'col')
- new_decoder_wide_weight: float32 [384, 3072], P('row', 'col')
- new_decoder_wide_first: float32 [384, 3072], P('row', 'col')
- new_decoder_wide_second: float32 [384, 3072], P('row', 'col')
- new_decoder_rows_weight: float32 [2304, 384], P('row', 'col')
- new_decoder_rows_first: float32 [2304, 384], P('row', 'col')
- new_decoder_rows_second: float32 [2304, 384], P('row', 'col')
- new_pixel_head_weight: float32 [384, 1536], replicated
- new_pixel_head_first: float32 [384, 1536], replicated
- new_pixel_head_second: float32 [384, 1536], replicated
- new_vectors_weight: float32 [5376], replicated
- new_vectors_first: float32 [5376], replicated
- new_vectors_second: float32 [5376], replicated
The draws below stay inside these ranges and needn't reach their ends.
Inputs may be any that keep to these rules, and one draw needn't show every extreme that they name: Each row of tube_order is a permutation of the tube numbers of its clip; its first 157 entries are the visible tubes.
All inputs are finite; a program needn't handle non-finite values.
Results may differ from the reference program's by a relative error of at most 0.006.
The reference program's roundings to bfloat16 on the way count: a program that leaves them out, or rounds other values in their place, can miss the bound.
Values may be sent and summed in bfloat16 or wider, within the bound.
No kernel may reach another device: no remote copies, remote signals or barrier semaphores. Data moves between devices by JAX's collectives and lax.ppermute only.
A program may use at most 640 MiB of HBM per device.

```python
import math
import jax
import jax.numpy as jnp
from jax import lax

D = 768
HEADS = 12
HDIM = 64
FF = 3072
DD = 384
DHEADS = 6
DFF = 1536
PIX = 1536
L = 2
NTUBE = 1568
NVIS = 157
CLIPS = 64
NMASK = 1411
WIDE = 6144
DWIDE = 3072
DROWS = 2304
NVEC = 5376


def levels(stream_key, shape, cuts, low, largest):
    def one(position, shards_of):
        steps = jax.random.uniform(jax.random.fold_in(jax.random.fold_in(stream_key, 6), position), (shards_of,), jnp.float32, low / len(cuts), largest / len(cuts))
        return jnp.repeat(jnp.exp(steps), shape[position] // shards_of).reshape((-1,) + (1,) * (len(shape) - position - 1))

    level = one(*cuts[0])
    for cut in cuts[1:]:
        level = level * one(*cut)
    return level


def gaussian(own_key, dims, deviation, bound, cuts=(), held_as=jnp.bfloat16):
    entries = jax.random.normal(own_key, dims, jnp.float32) * deviation
    if len(cuts) > 0:
        entries = levels(own_key, dims, cuts, -0.22, 0.18) * entries
    return jnp.clip(entries, min=-bound, max=bound).astype(held_as)


def setup_inputs(seed: int = 0) -> dict:
    seeds = jax.random.split(jax.random.key(seed), 25)
    return {
        "tubes": gaussian(seeds[0], (CLIPS, NTUBE, PIX), 1.0, 6.0, ((0, 32),)),
        "tube_order": jax.vmap(lambda own: jax.random.permutation(own, NTUBE))(jax.random.split(seeds[1], CLIPS)).reshape((CLIPS, NTUBE)).astype(jnp.int32),
        "step_count": jax.random.randint(seeds[2], (1,), 2, 21).astype(jnp.int32),
        "embed_weight": gaussian(seeds[3], (PIX, D), PIX ** -0.5, 0.15625, ((0, 4), (1, 8)), jnp.float32),
        "embed_first": gaussian(seeds[4], (PIX, D), (3 * (PIX * PIX * CLIPS * NMASK) ** -0.5), 9.1552734375e-05, ((0, 4), (1, 8)), jnp.float32),
        "embed_second": jnp.clip(jnp.exp(math.log(3.379427016003689e-10) - 2.7725887 * jax.random.uniform(seeds[5], (PIX, D), jnp.float32) ** levels(seeds[5], (PIX, D), ((0, 4), (1, 8)), -0.2, 0.2)), 2.1121418850023055e-11, 3.379427016003689e-10),
        "encoder_wide_weight": gaussian(seeds[6], (L, D, WIDE), D ** -0.5, 0.21875, ((1, 4), (2, 8)), jnp.float32),
        "encoder_wide_first": gaussian(seeds[7], (L, D, WIDE), (3 * (PIX * PIX * CLIPS * NMASK) ** -0.5), 9.1552734375e-05, ((1, 4), (2, 8)), jnp.float32),
        "encoder_wide_second": jnp.clip(jnp.exp(math.log(3.379427016003689e-10) - 2.7725887 * jax.random.uniform(seeds[8], (L, D, WIDE), jnp.float32) ** levels(seeds[8], (L, D, WIDE), ((1, 4), (2, 8)), -0.2, 0.2)), 2.1121418850023055e-11, 3.379427016003689e-10),
        "encoder_down_weight": gaussian(seeds[9], (L, FF, D), FF ** -0.5, 0.109375, ((1, 4), (2, 8)), jnp.float32),
        "encoder_down_first": gaussian(seeds[10], (L, FF, D), (3 * (PIX * PIX * CLIPS * NMASK) ** -0.5), 9.1552734375e-05, ((1, 4), (2, 8)), jnp.float32),
        "encoder_down_second": jnp.clip(jnp.exp(math.log(3.379427016003689e-10) - 2.7725887 * jax.random.uniform(seeds[11], (L, FF, D), jnp.float32) ** levels(seeds[11], (L, FF, D), ((1, 4), (2, 8)), -0.2, 0.2)), 2.1121418850023055e-11, 3.379427016003689e-10),
        "decoder_wide_weight": gaussian(seeds[12], (DD, DWIDE), DD ** -0.5, 0.3125, ((0, 4), (1, 8)), jnp.float32),
        "decoder_wide_first": gaussian(seeds[13], (DD, DWIDE), (3 * (PIX * PIX * CLIPS * NMASK) ** -0.5), 9.1552734375e-05, ((0, 4), (1, 8)), jnp.float32),
        "decoder_wide_second": jnp.clip(jnp.exp(math.log(3.379427016003689e-10) - 2.7725887 * jax.random.uniform(seeds[14], (DD, DWIDE), jnp.float32) ** levels(seeds[14], (DD, DWIDE), ((0, 4), (1, 8)), -0.2, 0.2)), 2.1121418850023055e-11, 3.379427016003689e-10),
        "decoder_rows_weight": gaussian(seeds[15], (DROWS, DD), DFF ** -0.5, 0.15625, ((0, 4), (1, 8)), jnp.float32),
        "decoder_rows_first": gaussian(seeds[16], (DROWS, DD), (3 * (PIX * PIX * CLIPS * NMASK) ** -0.5), 9.1552734375e-05, ((0, 4), (1, 8)), jnp.float32),
        "decoder_rows_second": jnp.clip(jnp.exp(math.log(3.379427016003689e-10) - 2.7725887 * jax.random.uniform(seeds[17], (DROWS, DD), jnp.float32) ** levels(seeds[17], (DROWS, DD), ((0, 4), (1, 8)), -0.2, 0.2)), 2.1121418850023055e-11, 3.379427016003689e-10),
        "pixel_head_weight": gaussian(seeds[18], (DD, PIX), DD ** -0.5, 0.3125, (), jnp.float32),
        "pixel_head_first": gaussian(seeds[19], (DD, PIX), (3 * (PIX * PIX * CLIPS * NMASK) ** -0.5), 9.1552734375e-05, (), jnp.float32),
        "pixel_head_second": jnp.clip(jnp.exp(jax.random.uniform(seeds[20], (DD, PIX), jnp.float32, math.log(2.1121418850023055e-11), math.log(3.379427016003689e-10))), 2.1121418850023055e-11, 3.379427016003689e-10),
        "vectors_weight": jnp.clip(1.0 + 0.1 * jax.random.normal(seeds[21], (NVEC,), jnp.float32), 0.5, 1.5),
        "vectors_first": gaussian(seeds[22], (NVEC,), (3 * (PIX * PIX * CLIPS * NMASK) ** -0.5), 9.1552734375e-05, (), jnp.float32),
        "vectors_second": jnp.clip(jnp.exp(jax.random.uniform(seeds[23], (NVEC,), jnp.float32, math.log(2.1121418850023055e-11), math.log(3.379427016003689e-10))), 2.1121418850023055e-11, 3.379427016003689e-10),
    }


@jax.custom_vjp
def low(v):
    return lax.optimization_barrier(v.astype(jnp.bfloat16)).astype(jnp.float32)

@jax.custom_vjp
def low_back(v):
    return v

def low_keep(v):
    return (low(v), None)

def low_pass(kept, grad):
    return (grad,)

def back_keep(v):
    return (v, None)

def back_low(kept, grad):
    return (low(grad),)
low.defvjp(low_keep, low_pass)
low_back.defvjp(back_keep, back_low)
highest = lax.Precision.HIGHEST
beta_first = 0.5
beta_second = 0.5
adam_epsilon = 1e-08
decay_factor = 0.05
norm_epsilon = 1e-06

def product(left, right):
    return jnp.dot(left, right, precision=highest)

def round_both(value):
    return low(low_back(value))

def sinusoid(count, width):
    places = jnp.arange(count, dtype=jnp.float32)[:, None]
    columns = jnp.arange(width // 2, dtype=jnp.float32)[None, :]
    angles = places * jnp.exp(columns * (-2.0 * jnp.log(10000.0) / width))
    return jnp.concatenate([jnp.sin(angles), jnp.cos(angles)], axis=1)

def layer_norm(values, gain):
    average = lax.optimization_barrier(jnp.mean(values, axis=-1, keepdims=True))
    centred = values - average
    spread = lax.optimization_barrier(jnp.mean(centred * centred, axis=-1, keepdims=True))
    return centred * lax.rsqrt(spread + norm_epsilon) * gain

def attention(packed, heads):
    length = packed.shape[0]
    width = packed.shape[1] // 3
    queries = packed[:, :width].reshape(length, heads, HDIM)
    keys = packed[:, width:2 * width].reshape(length, heads, HDIM)
    values = packed[:, 2 * width:].reshape(length, heads, HDIM)
    scores = low_back(jnp.einsum('qhd,khd->hqk', queries, keys, precision=highest) * HDIM ** (-0.5))
    weights = low(jax.nn.softmax(scores, axis=-1))
    mixed = jnp.einsum('hqk,khd->qhd', weights, values, precision=highest)
    return mixed.reshape(length, width)

def layer(stream, wide, down, gain_first, gain_second, heads):
    width = stream.shape[1]
    normed = low(layer_norm(stream, gain_first))
    packed = round_both(product(normed, wide[:, :3 * width]))
    mixed = round_both(attention(packed, heads))
    stream = stream + low_back(product(mixed, wide[:, 3 * width:4 * width]))
    normed = low(layer_norm(stream, gain_second))
    hidden = low_back(product(normed, wide[:, 4 * width:]))
    activated = low(jax.nn.gelu(hidden, approximate=False))
    return stream + low_back(product(activated, down))

def clip_loss(params, tube, order):
    embed, enc_wide, enc_down, dec_wide, dec_rows, head = [low(item) for item in params[:6]]
    vectors = params[6]
    pixels = tube.astype(jnp.float32)
    visible = order[:NVIS]
    masked = order[NVIS:]
    stream = low_back(product(pixels[visible], embed)) + sinusoid(NTUBE, D)[visible]
    for depth in range(L):
        stream = layer(stream, enc_wide[depth], enc_down[depth], vectors[2 * depth * D:(2 * depth + 1) * D], vectors[(2 * depth + 1) * D:(2 * depth + 2) * D], HEADS)
    base = (2 * L + 1) * D
    normed = low(layer_norm(stream, vectors[2 * L * D:base]))
    bridged = low_back(product(normed, dec_rows[DFF:]))
    places = sinusoid(NTUBE, DD)
    token_mask = vectors[base + 3 * DD:base + 4 * DD]
    decoded = jnp.concatenate([bridged + places[visible], token_mask[None, :] + places[masked]], axis=0)
    decoded = layer(decoded, dec_wide, dec_rows[:DFF], vectors[base:base + DD], vectors[base + DD:base + 2 * DD], DHEADS)
    normed = low(layer_norm(decoded[NVIS:], vectors[base + 2 * DD:base + 3 * DD]))
    predicted = low_back(product(normed, head))
    target = layer_norm(pixels[masked], 1.0)
    error = predicted - target
    return jnp.sum(error * error) * (1.0 / (CLIPS * NMASK * PIX))

def adam_update(master, moment, second, grad, rate, decay, count):
    moment = beta_first * moment + (1.0 - beta_first) * grad
    second = beta_second * second + (1.0 - beta_second) * grad * grad
    first_hat = moment / (1.0 - beta_first ** count)
    second_hat = second / (1.0 - beta_second ** count)
    master = master - rate * (first_hat / (jnp.sqrt(second_hat) + adam_epsilon) + decay * master)
    return (master, moment, second)

def reference(tubes, tube_order, step_count, embed_weight, embed_first, embed_second, encoder_wide_weight, encoder_wide_first, encoder_wide_second, encoder_down_weight, encoder_down_first, encoder_down_second, decoder_wide_weight, decoder_wide_first, decoder_wide_second, decoder_rows_weight, decoder_rows_first, decoder_rows_second, pixel_head_weight, pixel_head_first, pixel_head_second, vectors_weight, vectors_first, vectors_second):
    params = (embed_weight, encoder_wide_weight, encoder_down_weight, decoder_wide_weight, decoder_rows_weight, pixel_head_weight, vectors_weight)
    firsts = (embed_first, encoder_wide_first, encoder_down_first, decoder_wide_first, decoder_rows_first, pixel_head_first, vectors_first)
    seconds = (embed_second, encoder_wide_second, encoder_down_second, decoder_wide_second, decoder_rows_second, pixel_head_second, vectors_second)

    def one_clip(carry, inputs):
        total, grads = carry
        value, pullback = jax.vjp(lambda chosen: clip_loss(chosen, inputs[0], inputs[1]), params)
        delta, = pullback(jnp.ones((), jnp.float32))
        return ((total + value, jax.tree.map(jnp.add, grads, delta)), None)
    start = (jnp.zeros((), jnp.float32), jax.tree.map(jnp.zeros_like, params))
    (loss, grads), _ = lax.scan(one_clip, start, (tubes, tube_order))
    count = step_count[0].astype(jnp.float32)
    rates = (PIX ** (-0.5), D ** (-0.5), FF ** (-0.5), DD ** (-0.5), DFF ** (-0.5), DD ** (-0.5), 0.1)
    decays = (decay_factor,) * 6 + (0.0,)
    results = [loss]
    for index in range(7):
        results.extend(adam_update(params[index], firsts[index], seconds[index], grads[index], rates[index], decays[index], count))
    return tuple(results)
```

```python
import jax
import jax.numpy as jnp
from jax import lax
from jax.sharding import PartitionSpec as P

D = 768
HEADS = 12
HDIM = 64
FF = 3072
DD = 384
DHEADS = 6
DFF = 1536
PIX = 1536
L = 2
NTUBE = 1568
NVIS = 157
NMASK = 1411


beta_first = 0.5
beta_second = 0.5
adam_epsilon = 1e-08
decay_factor = 0.05
norm_epsilon = 1e-06


def product(left, right):
    return jnp.dot(left, right, preferred_element_type=jnp.float32)


def product_left(left, right):
    return lax.dot_general(
        left, right, (((0,), (0,)), ((), ())), preferred_element_type=jnp.float32
    )


def product_right(left, right):
    return lax.dot_general(
        left, right, (((1,), (1,)), ((), ())), preferred_element_type=jnp.float32
    )


def sinusoid(count, width):
    places = jnp.arange(count, dtype=jnp.float32)[:, None]
    columns = jnp.arange(width // 2, dtype=jnp.float32)[None, :]
    angles = places * jnp.exp(columns * (-2.0 * jnp.log(10000.0) / width))
    return jnp.concatenate([jnp.sin(angles), jnp.cos(angles)], axis=1)


def layer_norm(values, gain):
    average = jnp.mean(values, axis=-1, keepdims=True)
    centred = values - average
    spread = jnp.mean(centred * centred, axis=-1, keepdims=True)
    return centred * lax.rsqrt(spread + norm_epsilon) * gain


def gelu_exact(values):
    return jax.nn.gelu(values, approximate=False)


def split_heads(packed, heads):
    length = packed.shape[0]
    width = packed.shape[1] // 3
    queries = packed[:, :width].reshape(length, heads, HDIM)
    keys = packed[:, width : 2 * width].reshape(length, heads, HDIM)
    values = packed[:, 2 * width :].reshape(length, heads, HDIM)
    blocks = 2 if length >= 1024 and length % 2 == 0 else 1
    return (queries, keys, values, blocks, length // blocks)


def attend(packed, heads):
    queries, keys, values, blocks, size = split_heads(packed, heads)
    scale = HDIM ** (-0.5)
    outputs = []
    totals = []
    for block in range(blocks):
        chosen = queries[block * size : (block + 1) * size]
        scores = (
            jnp.einsum("qhd,khd->hqk", chosen, keys, preferred_element_type=jnp.float32) * scale
        )
        largest = jnp.max(scores, axis=-1, keepdims=True)
        raised = jnp.exp(scores - largest)
        summed = jnp.sum(raised, axis=-1, keepdims=True)
        weights = (raised / summed).astype(jnp.bfloat16)
        outputs.append(
            jnp.einsum("hqk,khd->qhd", weights, values, preferred_element_type=jnp.float32)
        )
        totals.append(largest + jnp.log(summed))
    mixed = jnp.concatenate(outputs, axis=0)
    return (mixed.reshape(packed.shape[0], -1).astype(jnp.bfloat16), totals)


def attend_back(packed, totals, grad_mixed, heads):
    queries, keys, values, blocks, size = split_heads(packed, heads)
    length = packed.shape[0]
    scale = HDIM ** (-0.5)
    grad_out = grad_mixed.reshape(length, heads, HDIM)
    grad_keys = jnp.zeros(keys.shape, jnp.float32)
    grad_values = jnp.zeros(values.shape, jnp.float32)
    grad_queries = []
    for block in range(blocks):
        lower = block * size
        chosen = queries[lower : lower + size]
        chosen_grad = grad_out[lower : lower + size]
        scores = (
            jnp.einsum("qhd,khd->hqk", chosen, keys, preferred_element_type=jnp.float32) * scale
        )
        probs = jnp.exp(scores - totals[block])
        grad_probs = jnp.einsum(
            "qhd,khd->hqk", chosen_grad, values, preferred_element_type=jnp.float32
        )
        inner = jnp.sum(probs * grad_probs, axis=-1, keepdims=True)
        grad_scores = (probs * (grad_probs - inner)).astype(jnp.bfloat16)
        grad_queries.append(
            jnp.einsum("hqk,khd->qhd", grad_scores, keys, preferred_element_type=jnp.float32)
            * scale
        )
        grad_keys = (
            grad_keys
            + jnp.einsum("hqk,qhd->khd", grad_scores, chosen, preferred_element_type=jnp.float32)
            * scale
        )
        grad_values = grad_values + jnp.einsum(
            "hqk,qhd->khd",
            probs.astype(jnp.bfloat16),
            chosen_grad,
            preferred_element_type=jnp.float32,
        )
    combined = jnp.concatenate(
        [
            jnp.concatenate(grad_queries, axis=0).reshape(length, -1),
            grad_keys.reshape(length, -1),
            grad_values.reshape(length, -1),
        ],
        axis=1,
    )
    return combined.astype(jnp.bfloat16)


def layer_forward(stream, wide, down, gain_first, gain_second, heads):
    width = stream.shape[1]
    normed, back_first = jax.vjp(layer_norm, stream, gain_first)
    normed = normed.astype(jnp.bfloat16)
    packed = product(normed, wide[:, : 3 * width]).astype(jnp.bfloat16)
    mixed, totals = attend(packed, heads)
    middle = stream + product(mixed, wide[:, 3 * width : 4 * width])
    second, back_second = jax.vjp(layer_norm, middle, gain_second)
    second = second.astype(jnp.bfloat16)
    hidden = product(second, wide[:, 4 * width :])
    activated, back_gelu = jax.vjp(gelu_exact, hidden)
    activated = activated.astype(jnp.bfloat16)
    output = middle + product_right(activated, down)
    return (
        output,
        (back_first, normed, packed, mixed, totals, back_second, second, back_gelu, activated),
    )


def layer_backward(grad_stream, wide, down, kept, heads):
    back_first, normed, packed, mixed, totals, back_second, second, back_gelu, activated = kept
    width = grad_stream.shape[1]
    grad_branch = grad_stream.astype(jnp.bfloat16)
    grad_down = product_left(grad_branch, activated)
    grad_hidden = back_gelu(product(grad_branch, down))[0].astype(jnp.bfloat16)
    grad_up = product_left(second, grad_hidden)
    grad_middle, grad_gain_second = back_second(product_right(grad_hidden, wide[:, 4 * width :]))
    grad_middle = grad_stream + grad_middle
    grad_attend = grad_middle.astype(jnp.bfloat16)
    grad_output = product_left(mixed, grad_attend)
    grad_mixed = product_right(grad_attend, wide[:, 3 * width : 4 * width]).astype(jnp.bfloat16)
    grad_packed = attend_back(packed, totals, grad_mixed, heads)
    grad_qkv = product_left(normed, grad_packed)
    grad_before, grad_gain_first = back_first(product_right(grad_packed, wide[:, : 3 * width]))
    grad_wide = jnp.concatenate([grad_qkv, grad_output, grad_up], axis=1)
    return (grad_middle + grad_before, grad_wide, grad_down, grad_gain_first, grad_gain_second)


def clip_grads(weights, vectors, tube, order, inverse):
    embed, enc_wide, enc_down, dec_wide, dec_rows, head = weights
    visible = order[:NVIS]
    masked = order[NVIS:]
    base = (2 * L + 1) * D
    seen = jnp.take(tube, visible, axis=0)
    stream = product_right(seen, embed) + jnp.take(sinusoid(NTUBE, D), visible, axis=0)
    kept_layers = []
    for depth in range(L):
        stream, kept = layer_forward(
            stream,
            enc_wide[depth],
            enc_down[depth],
            vectors[2 * depth * D : (2 * depth + 1) * D],
            vectors[(2 * depth + 1) * D : (2 * depth + 2) * D],
            HEADS,
        )
        kept_layers.append(kept)
    normed, back_encoder = jax.vjp(layer_norm, stream, vectors[2 * L * D : base])
    normed = normed.astype(jnp.bfloat16)
    bridge = dec_rows[:, DFF:]
    bridged = product_right(normed, bridge)
    places = sinusoid(NTUBE, DD)
    token_mask = vectors[base + 3 * DD : base + 4 * DD]
    decoded = jnp.concatenate(
        [
            bridged + jnp.take(places, visible, axis=0),
            token_mask[None, :] + jnp.take(places, masked, axis=0),
        ],
        axis=0,
    )
    decoded, kept_decoder = layer_forward(
        decoded,
        dec_wide,
        dec_rows[:, :DFF],
        vectors[base : base + DD],
        vectors[base + DD : base + 2 * DD],
        DHEADS,
    )
    final, back_final = jax.vjp(layer_norm, decoded[NVIS:], vectors[base + 2 * DD : base + 3 * DD])
    final = final.astype(jnp.bfloat16)
    predicted = product(final, head)
    target = layer_norm(jnp.take(tube, masked, axis=0).astype(jnp.float32), 1.0)
    error = predicted - target
    loss_value = jnp.sum(error * error) * inverse
    grad_predicted = (2.0 * inverse * error).astype(jnp.bfloat16)
    grad_head = product_left(final, grad_predicted)
    grad_tail, grad_gain_final = back_final(product_right(grad_predicted, head))
    grad_decoded = jnp.concatenate([jnp.zeros((NVIS, DD), jnp.float32), grad_tail], axis=0)
    grad_decoded, grad_dec_wide, grad_dec_down, dec_gain_first, dec_gain_second = layer_backward(
        grad_decoded, dec_wide, dec_rows[:, :DFF], kept_decoder, DHEADS
    )
    grad_token = jnp.sum(grad_decoded[NVIS:], axis=0)
    grad_bridged = grad_decoded[:NVIS].astype(jnp.bfloat16)
    grad_bridge = product_left(grad_bridged, normed)
    grad_stream, grad_gain_encoder = back_encoder(product(grad_bridged, bridge))
    wide_grads = [None] * L
    down_grads = [None] * L
    gain_grads = [None] * L
    for depth in reversed(range(L)):
        grad_stream, wide_grads[depth], down_grads[depth], first_gain, second_gain = layer_backward(
            grad_stream, enc_wide[depth], enc_down[depth], kept_layers[depth], HEADS
        )
        gain_grads[depth] = jnp.concatenate([first_gain, second_gain])
    grad_embed = product_left(grad_stream.astype(jnp.bfloat16), seen)
    grad_vectors = jnp.concatenate(
        gain_grads
        + [grad_gain_encoder, dec_gain_first, dec_gain_second, grad_gain_final, grad_token]
    )
    grads = (
        grad_embed,
        tuple(wide_grads),
        tuple(down_grads),
        grad_dec_wide,
        jnp.concatenate([grad_dec_down, grad_bridge], axis=1),
        grad_head,
        grad_vectors,
    )
    return (loss_value, grads)


def pack_block(block, width):
    height, breadth = block.shape[-2:]
    lead = block.shape[:-2]
    if breadth == width:
        return block
    if width % breadth == 0 and height % (width // breadth) == 0:
        times = width // breadth
        split = block.reshape(lead + (times, height // times, breadth))
        return jnp.concatenate([split[..., part, :, :] for part in range(times)], axis=-1)
    return block.reshape(lead + (height * breadth // width, width))


def unpack_block(block, height, breadth):
    width = block.shape[-1]
    lead = block.shape[:-2]
    if breadth == width:
        return block
    if width % breadth == 0 and height % (width // breadth) == 0:
        times = width // breadth
        return jnp.concatenate(
            [block[..., part * breadth : (part + 1) * breadth] for part in range(times)], axis=-2
        )
    return block.reshape(lead + (height, breadth))


def group_width(shapes):
    return next(iter(shapes))[1]


def gather_group(pieces, rows, cols):
    width = group_width([block.shape for block, _ in pieces.values()])
    packed = jnp.concatenate([pack_block(block, width) for block, _ in pieces.values()], axis=0)
    everything = lax.all_gather(packed, ("row", "col"), axis=0)
    full = {}
    start = 0
    for name, (block, flipped) in pieces.items():
        height, breadth = block.shape
        count = height * breadth // width
        part = unpack_block(everything[:, start : start + count], height, breadth)
        part = part.reshape(rows, cols, height, breadth)
        start += count
        if flipped:
            full[name] = part.transpose(1, 2, 0, 3).reshape(cols * height, rows * breadth)
        else:
            full[name] = part.transpose(0, 2, 1, 3).reshape(rows * height, cols * breadth)
    return full


def scatter_group(pieces, rows, cols):
    width = group_width([shape for _, shape, _ in pieces.values()])
    blocks = []
    for whole, (height, breadth), flipped in pieces.values():
        whole = whole.astype(jnp.bfloat16)
        if flipped:
            part = whole.reshape(cols, height, rows, breadth).transpose(2, 0, 1, 3)
        else:
            part = whole.reshape(rows, height, cols, breadth).transpose(0, 2, 1, 3)
        blocks.append(pack_block(part.reshape(rows * cols, height, breadth), width))
    packed = jnp.concatenate(blocks, axis=1)
    total = lax.psum_scatter(packed, ("row", "col"), scatter_dimension=0)
    mine = {}
    start = 0
    for name, (_, (height, breadth), _) in pieces.items():
        count = height * breadth // width
        mine[name] = unpack_block(total[start : start + count], height, breadth).astype(
            jnp.float32
        )
        start += count
    return mine


def adam_update(master, moment, second, grad, rate, decay, count):
    moment = beta_first * moment + (1.0 - beta_first) * grad
    second = beta_second * second + (1.0 - beta_second) * grad * grad
    first_hat = moment / (1.0 - beta_first**count)
    second_hat = second / (1.0 - beta_second**count)
    master = master - rate * (first_hat / (jnp.sqrt(second_hat) + adam_epsilon) + decay * master)
    return (master, moment, second)


def shards(
    tubes,
    tube_order,
    step_count,
    embed_weight,
    embed_first,
    embed_second,
    encoder_wide_weight,
    encoder_wide_first,
    encoder_wide_second,
    encoder_down_weight,
    encoder_down_first,
    encoder_down_second,
    decoder_wide_weight,
    decoder_wide_first,
    decoder_wide_second,
    decoder_rows_weight,
    decoder_rows_first,
    decoder_rows_second,
    pixel_head_weight,
    pixel_head_first,
    pixel_head_second,
    vectors_weight,
    vectors_first,
    vectors_second,
):
    rows, cols = lax.axis_size("row"), lax.axis_size("col")
    low = jnp.bfloat16
    pieces = {
        "embed": (embed_weight.astype(low).T, True),
        "dec_wide": (decoder_wide_weight.astype(low), False),
        "dec_rows": (decoder_rows_weight.astype(low).T, True),
    }
    for depth in range(L):
        pieces["wide%d" % depth] = (encoder_wide_weight[depth].astype(low), False)
        pieces["down%d" % depth] = (encoder_down_weight[depth].astype(low).T, True)
    groups = (("wide0", "down0", "embed"), ("wide1", "down1", "dec_wide", "dec_rows"))
    order = [name for group in groups for name in group]
    full = gather_group({name: pieces[name] for name in order}, rows, cols)
    whole = (
        full["embed"],
        tuple(full["wide%d" % depth] for depth in range(L)),
        tuple(full["down%d" % depth] for depth in range(L)),
        full["dec_wide"],
        full["dec_rows"],
    )
    weights = tuple(whole) + (pixel_head_weight.astype(jnp.bfloat16),)
    inverse = 1.0 / (tubes.shape[0] * lax.axis_size("row") * lax.axis_size("col") * NMASK * PIX)
    loss_local = jnp.zeros((), jnp.float32)
    totals = None
    for clip in range(tubes.shape[0]):
        value, grads = clip_grads(weights, vectors_weight, tubes[clip], tube_order[clip], inverse)
        loss_local = loss_local + value
        totals = grads if totals is None else jax.tree.map(jnp.add, totals, grads)
    summed = {"embed": totals[0], "dec_wide": totals[3], "dec_rows": totals[4]}
    for depth in range(L):
        summed["wide%d" % depth] = totals[1][depth]
        summed["down%d" % depth] = totals[2][depth]
    mine = {}
    for group in (groups[1], groups[0]):
        mine.update(
            scatter_group(
                {name: (summed[name], pieces[name][0].shape, pieces[name][1]) for name in group},
                rows,
                cols,
            )
        )
    owned = (
        mine["embed"].T,
        jnp.stack([mine["wide%d" % depth] for depth in range(L)]),
        jnp.stack([mine["down%d" % depth].T for depth in range(L)]),
        mine["dec_wide"],
        mine["dec_rows"].T,
    )
    loss, grad_head, grad_vectors = lax.psum((loss_local, totals[5], totals[6]), ("row", "col"))
    grads = tuple(owned) + (grad_head, grad_vectors)
    masters = (
        embed_weight,
        encoder_wide_weight,
        encoder_down_weight,
        decoder_wide_weight,
        decoder_rows_weight,
        pixel_head_weight,
        vectors_weight,
    )
    firsts = (
        embed_first,
        encoder_wide_first,
        encoder_down_first,
        decoder_wide_first,
        decoder_rows_first,
        pixel_head_first,
        vectors_first,
    )
    seconds = (
        embed_second,
        encoder_wide_second,
        encoder_down_second,
        decoder_wide_second,
        decoder_rows_second,
        pixel_head_second,
        vectors_second,
    )
    count = step_count[0].astype(jnp.float32)
    rates = (
        PIX ** (-0.5),
        D ** (-0.5),
        FF ** (-0.5),
        DD ** (-0.5),
        DFF ** (-0.5),
        DD ** (-0.5),
        0.1,
    )
    decays = (decay_factor,) * 6 + (0.0,)
    results = [loss]
    for index in range(7):
        results.extend(
            adam_update(
                masters[index],
                firsts[index],
                seconds[index],
                grads[index],
                rates[index],
                decays[index],
                count,
            )
        )
    return tuple(results)


def solution(mesh):
    placed = (
        P(("row", "col"), None, None),
        P(("row", "col"), None),
        P(),
        P("row", "col"),
        P("row", "col"),
        P("row", "col"),
        P(None, "row", "col"),
        P(None, "row", "col"),
        P(None, "row", "col"),
        P(None, "row", "col"),
        P(None, "row", "col"),
        P(None, "row", "col"),
        P("row", "col"),
        P("row", "col"),
        P("row", "col"),
        P("row", "col"),
        P("row", "col"),
        P("row", "col"),
        P(),
        P(),
        P(),
        P(),
        P(),
        P(),
    )
    return jax.shard_map(
        shards,
        mesh=mesh,
        in_specs=placed,
        out_specs=(
            P(),
            P("row", "col"),
            P("row", "col"),
            P("row", "col"),
            P(None, "row", "col"),
            P(None, "row", "col"),
            P(None, "row", "col"),
            P(None, "row", "col"),
            P(None, "row", "col"),
            P(None, "row", "col"),
            P("row", "col"),
            P("row", "col"),
            P("row", "col"),
            P("row", "col"),
            P("row", "col"),
            P("row", "col"),
            P(),
            P(),
            P(),
            P(),
            P(),
            P(),
        ),
        check_vma=False,
    )
```

```python
import jax
import jax.numpy as jnp
from jax import lax
from jax.experimental import pallas as pl
from jax.experimental.pallas import tpu as pltpu
from jax.sharding import PartitionSpec as P

D = 768
HEADS = 12
HDIM = 64
FF = 3072
DD = 384
DHEADS = 6
DFF = 1536
PIX = 1536
L = 2
NTUBE = 1568
NVIS = 157
NMASK = 1411
NPAD = 160
PAIR = 2 * HDIM


beta_first = 0.5
beta_second = 0.5
adam_epsilon = 1e-08
decay_factor = 0.05
norm_epsilon = 1e-06


def product(left, right):
    return jnp.dot(left, right, preferred_element_type=jnp.float32)


def product_left(left, right):
    return lax.dot_general(
        left, right, (((0,), (0,)), ((), ())), preferred_element_type=jnp.float32
    )


def product_right(left, right):
    return lax.dot_general(
        left, right, (((1,), (1,)), ((), ())), preferred_element_type=jnp.float32
    )


def sinusoid(places, width):
    columns = jnp.arange(width // 2, dtype=jnp.float32)[None, :]
    angles = places[:, None] * jnp.exp(columns * (-2.0 * jnp.log(10000.0) / width))
    return jnp.concatenate([jnp.sin(angles), jnp.cos(angles)], axis=1)


def layer_norm(values, gain):
    average = jnp.mean(values, axis=-1, keepdims=True)
    centred = values - average
    spread = jnp.mean(centred * centred, axis=-1, keepdims=True)
    return centred * lax.rsqrt(spread + norm_epsilon) * gain


def gelu_parts(values):
    below = 0.5 * (1.0 + lax.erf(values * 0.5**0.5))
    density = jnp.exp(-0.5 * values * values) * (2.0 * jnp.pi) ** (-0.5)
    return (values * below, below + values * density)


def contract(left, right, left_dim, right_dim):
    return lax.dot_general(
        left,
        right,
        (((left_dim,), (right_dim,)), ((), ())),
        preferred_element_type=jnp.float32,
    )


def lane_halves(shape):
    lane = lax.broadcasted_iota(jnp.int32, shape, 1)
    return (lane < HDIM, lane >= HDIM)


def attend_kernel(valid, q_ref, k_ref, v_ref, o_ref, t_ref):
    queries = q_ref[...] * jnp.bfloat16(HDIM**-0.5)
    halves = lane_halves(queries.shape)
    keys = k_ref[...]
    values = v_ref[...]
    outputs = []
    totals = []
    for half in halves:
        chosen = jnp.where(half, queries, jnp.bfloat16(0))
        scores = contract(chosen, keys, 1, 1)
        if valid < keys.shape[0]:
            known = lax.broadcasted_iota(jnp.int32, scores.shape, 1) < valid
            scores = jnp.where(known, scores, -3e38)
        largest = jnp.max(scores, axis=1, keepdims=True)
        raised = jnp.exp(scores - largest)
        summed = jnp.sum(raised, axis=1, keepdims=True)
        outputs.append(contract(raised.astype(jnp.bfloat16), values, 1, 0) / summed)
        totals.append(largest + jnp.log(summed))
    o_ref[...] = jnp.where(halves[0], outputs[0], outputs[1]).astype(jnp.bfloat16)
    t_ref[...] = jnp.where(halves[0], totals[0], totals[1])


def attend_back_kernel(
    valid, q_ref, k_ref, v_ref, t_ref, g_ref, dq_ref, dk_ref, dv_ref, ak_ref, av_ref
):
    step = pl.program_id(2)

    @pl.when(step == 0)
    def _():
        ak_ref[...] = jnp.zeros_like(ak_ref)
        av_ref[...] = jnp.zeros_like(av_ref)

    queries = q_ref[...] * jnp.bfloat16(HDIM**-0.5)
    keys = k_ref[...]
    values = v_ref[...]
    grads = g_ref[...]
    totals = t_ref[...]
    halves = lane_halves(queries.shape)
    parts = []
    for index, half in enumerate(halves):
        chosen = jnp.where(half, queries, jnp.bfloat16(0))
        grad = jnp.where(half, grads, jnp.bfloat16(0))
        scores = contract(chosen, keys, 1, 1)
        if valid < keys.shape[0]:
            known = lax.broadcasted_iota(jnp.int32, scores.shape, 1) < valid
            scores = jnp.where(known, scores, -3e38)
        probs = jnp.exp(scores - totals[:, index * HDIM : index * HDIM + 1])
        lifted = probs * contract(grad, values, 1, 1)
        inner = jnp.sum(lifted, axis=1, keepdims=True)
        grad_scores = (lifted - probs * inner).astype(jnp.bfloat16)
        parts.append(contract(grad_scores, keys, 1, 0))
        ak_ref[...] += contract(grad_scores, chosen, 0, 0)
        av_ref[...] += contract(probs.astype(jnp.bfloat16), grad, 0, 0)
    mixed = jnp.where(halves[0], parts[0], parts[1]) * HDIM ** (-0.5)
    dq_ref[...] = mixed.astype(jnp.bfloat16)

    @pl.when(step == pl.num_programs(2) - 1)
    def _():
        dk_ref[...] = ak_ref[...].astype(jnp.bfloat16)
        dv_ref[...] = av_ref[...].astype(jnp.bfloat16)


def attend(packed, clips, heads, valid, block):
    length = packed.shape[0] // clips
    pairs = heads // 2
    steps = length // block
    some = pl.BlockSpec((block, PAIR), lambda c, h, i: (c * steps + i, h))
    tall = packed.shape[0]
    return pl.pallas_call(
        lambda *refs: attend_kernel(valid, *refs),
        grid=(clips, pairs, steps),
        in_specs=[
            some,
            pl.BlockSpec((length, PAIR), lambda c, h, i: (c, pairs + h)),
            pl.BlockSpec((length, PAIR), lambda c, h, i: (c, 2 * pairs + h)),
        ],
        out_specs=[some, some],
        out_shape=[
            jax.ShapeDtypeStruct((tall, heads * HDIM), jnp.bfloat16),
            jax.ShapeDtypeStruct((tall, heads * HDIM), jnp.float32),
        ],
        cost_estimate=pl.CostEstimate(
            flops=16 * tall * length * heads * HDIM,
            bytes_accessed=12 * tall * heads * HDIM,
            transcendentals=tall * length * heads,
        ),
        name="attend",
    )(packed, packed, packed)


def attend_back(packed, totals, grads, clips, heads, valid, block):
    length = packed.shape[0] // clips
    pairs = heads // 2
    steps = length // block
    some = pl.BlockSpec((block, PAIR), lambda c, h, i: (c * steps + i, h))
    every = pl.BlockSpec((length, PAIR), lambda c, h, i: (c, h))
    tall = packed.shape[0]
    shape = jax.ShapeDtypeStruct((tall, heads * HDIM), jnp.bfloat16)
    return pl.pallas_call(
        lambda *refs: attend_back_kernel(valid, *refs),
        grid=(clips, pairs, steps),
        in_specs=[
            some,
            pl.BlockSpec((length, PAIR), lambda c, h, i: (c, pairs + h)),
            pl.BlockSpec((length, PAIR), lambda c, h, i: (c, 2 * pairs + h)),
            some,
            some,
        ],
        out_specs=[some, every, every],
        out_shape=[shape, shape, shape],
        scratch_shapes=[
            pltpu.VMEM((length, PAIR), jnp.float32),
            pltpu.VMEM((length, PAIR), jnp.float32),
        ],
        cost_estimate=pl.CostEstimate(
            flops=40 * tall * length * heads * HDIM,
            bytes_accessed=20 * tall * heads * HDIM,
            transcendentals=tall * length * heads,
        ),
        name="attend_back",
    )(packed, packed, packed, totals, grads)


def layer_forward(stream, wide, down, gain_first, gain_second, form):
    width = stream.shape[1]
    normed, back_first = jax.vjp(layer_norm, stream, gain_first)
    normed = normed.astype(jnp.bfloat16)
    packed = product(normed, wide[:, : 3 * width]).astype(jnp.bfloat16)
    mixed, totals = attend(packed, *form)
    middle = stream + product(mixed, wide[:, 3 * width : 4 * width])
    second, back_second = jax.vjp(layer_norm, middle, gain_second)
    second = second.astype(jnp.bfloat16)
    activated, slope = gelu_parts(product(second, wide[:, 4 * width :]))
    activated = activated.astype(jnp.bfloat16)
    slope = slope.astype(jnp.bfloat16)
    output = middle + product_right(activated, down)
    return (
        output,
        (back_first, normed, packed, mixed, totals, back_second, second, slope, activated),
    )


def layer_backward(grad_stream, wide, down, kept, form):
    back_first, normed, packed, mixed, totals, back_second, second, slope, activated = kept
    low = jnp.bfloat16
    width = grad_stream.shape[1]
    grad_branch = grad_stream.astype(low)
    grad_down = product_left(grad_branch, activated).astype(low)
    grad_hidden = (slope.astype(jnp.float32) * product(grad_branch, down)).astype(low)
    grad_up = product_left(second, grad_hidden).astype(low)
    grad_middle, grad_gain_second = back_second(product_right(grad_hidden, wide[:, 4 * width :]))
    grad_middle = grad_stream + grad_middle
    grad_attend = grad_middle.astype(low)
    grad_output = product_left(mixed, grad_attend).astype(low)
    grad_mixed = product_right(grad_attend, wide[:, 3 * width : 4 * width]).astype(low)
    grad_parts = attend_back(packed, totals, grad_mixed, *form)
    grad_packed = jnp.concatenate(grad_parts, axis=1)
    grad_qkv = product_left(normed, grad_packed).astype(low)
    grad_before, grad_gain_first = back_first(product_right(grad_packed, wide[:, : 3 * width]))
    grad_wide = (grad_qkv, grad_output, grad_up)
    return (grad_middle + grad_before, grad_wide, grad_down, grad_gain_first, grad_gain_second)


def all_grads(weights, head, vectors, tubes, orders, inverse, reduce_head, reduce_late):
    clips = tubes.shape[0]
    low = jnp.bfloat16
    base = (2 * L + 1) * D
    encoder_form = (clips, HEADS, NVIS, NPAD)
    decoder_form = (clips, DHEADS, NTUBE, NTUBE // 7)
    visible = jnp.pad(orders[:, :NVIS], ((0, 0), (0, NPAD - NVIS)), constant_values=-1)
    chosen = visible[:, :, None] == jnp.arange(NTUBE, dtype=jnp.int32)[None, None, :]
    chosen_low = chosen.astype(low)
    shown = jnp.any(chosen, axis=1)
    pixels = tubes.reshape(clips * NTUBE, PIX)
    seen = jnp.einsum("cvp,cpd->cvd", chosen_low, tubes, preferred_element_type=jnp.float32)
    seen = seen.astype(low).reshape(clips * NPAD, PIX)
    places = visible.reshape(-1).astype(jnp.float32)
    stream = product_right(seen, weights["embed"]) + sinusoid(places, D)
    kept_layers = []
    for depth in range(L):
        stream, kept = layer_forward(
            stream,
            weights["wide%d" % depth],
            weights["down%d" % depth],
            vectors[2 * depth * D : (2 * depth + 1) * D],
            vectors[(2 * depth + 1) * D : (2 * depth + 2) * D],
            encoder_form,
        )
        kept_layers.append(kept)
    normed, back_encoder = jax.vjp(layer_norm, stream, vectors[2 * L * D : base])
    normed = normed.astype(low)
    bridge = weights["dec_rows"][:, DFF:]
    bridged = product_right(normed, bridge).reshape(clips, NPAD, DD)
    placed = jnp.einsum(
        "cvp,cvd->cpd",
        chosen.astype(jnp.float32),
        bridged,
        precision=lax.Precision.HIGHEST,
        preferred_element_type=jnp.float32,
    )
    token_mask = vectors[base + 3 * DD : base + 4 * DD]
    table = sinusoid(jnp.arange(NTUBE, dtype=jnp.float32), DD)
    decoded = jnp.where(shown[:, :, None], placed, token_mask) + table[None]
    decoded = decoded.reshape(clips * NTUBE, DD)
    hidden_rows = jnp.logical_not(shown).reshape(-1, 1)
    decoded, kept_decoder = layer_forward(
        decoded,
        weights["dec_wide"],
        weights["dec_rows"][:, :DFF],
        vectors[base : base + DD],
        vectors[base + DD : base + 2 * DD],
        decoder_form,
    )
    final, back_final = jax.vjp(layer_norm, decoded, vectors[base + 2 * DD : base + 3 * DD])
    final = final.astype(low)
    target = layer_norm(pixels.astype(jnp.float32), 1.0)
    error = jnp.where(hidden_rows, product(final, head) - target, 0.0)
    loss_value = jnp.sum(error * error) * inverse
    grad_predicted = (2.0 * inverse * error).astype(low)
    grad_head = reduce_head(product_left(final, grad_predicted))
    grad_decoded, grad_gain_final = back_final(product_right(grad_predicted, head))
    grads = {}
    grad_decoded, grads["dec_wide"], grad_dec_down, dec_gain_first, dec_gain_second = (
        layer_backward(
            grad_decoded,
            weights["dec_wide"],
            weights["dec_rows"][:, :DFF],
            kept_decoder,
            decoder_form,
        )
    )
    grads["dec_wide"] = jnp.concatenate(grads["dec_wide"], axis=1)
    grad_decoded, grad_head = lax.optimization_barrier((grad_decoded, grad_head))
    grad_token = jnp.sum(jnp.where(hidden_rows, grad_decoded, 0.0), axis=0)
    grad_bridged = jnp.einsum(
        "cvp,cpd->cvd",
        chosen_low,
        grad_decoded.astype(low).reshape(clips, NTUBE, DD),
        preferred_element_type=jnp.float32,
    )
    grad_bridged = grad_bridged.astype(low).reshape(clips * NPAD, DD)
    grad_bridge = product_left(grad_bridged, normed).astype(low)
    grads["dec_rows"] = jnp.concatenate([grad_dec_down, grad_bridge], axis=1)
    grad_stream, grad_gain_encoder = back_encoder(product(grad_bridged, bridge))
    gain_grads = [None] * L
    mine = {}
    for depth in reversed(range(L)):
        grad_stream, grads["wide%d" % depth], grads["down%d" % depth], first_gain, second_gain = (
            layer_backward(
                grad_stream,
                weights["wide%d" % depth],
                weights["down%d" % depth],
                kept_layers[depth],
                encoder_form,
            )
        )
        gain_grads[depth] = jnp.concatenate([first_gain, second_gain])
        if depth == 0:
            grads["embed"] = product_left(grad_stream.astype(low), seen).astype(low)
        mine.update(reduce_late(grads, depth))
    grad_vectors = jnp.concatenate(
        gain_grads
        + [grad_gain_encoder, dec_gain_first, dec_gain_second, grad_gain_final, grad_token]
    )
    return (loss_value, mine, grad_head, grad_vectors)


BOTH = ("row", "col")


def exchange(value, bit):
    return lax.ppermute(value, BOTH, [(i, i ^ bit) for i in range(32)])


def rotate(value):
    return lax.ppermute(value, BOTH, [(i, (i & ~6) | ((i + 2) & 6)) for i in range(32)])


def own_place():
    row, col = lax.axis_index("row"), lax.axis_index("col")
    return {"y": row // 2, "x": row % 2, "z": col // 2, "c": col % 2}


BITS = {"y": 16, "x": 8, "c": 1}
GATHER_NAMES = ("yxcz", "xczy", "zcyx")
SCATTER_NAMES = ("cyxz", "cxzy", "czyx")
EXTENT = {"y": 2, "x": 2, "z": 4, "c": 2}


def set_block(total, block, start):
    return lax.dynamic_update_slice(total, block, (start, 0, 0))


def ordered_pair(own, name, place):
    other = exchange(own, BITS[name])
    first = place[name] == 0
    return jnp.concatenate([jnp.where(first, own, other), jnp.where(first, other, own)], axis=0)


def ring_blocks(own):
    blocks = [own]
    for _ in range(3):
        blocks.append(rotate(blocks[-1]))
    return blocks


def ring_gather(own, place):
    count = own.shape[0]
    total = jnp.zeros((4 * count,) + own.shape[1:], own.dtype)
    for hop, block in enumerate(ring_blocks(own)):
        total = set_block(total, block, (place["z"] - hop) % 4 * count)
    return total


def gather_chunk(own, form, place):
    own = own[None]
    y, x, z, c = (place[name] for name in "yxzc")
    if form == 0:
        near = ring_gather(own, place)
        aside = exchange(near, BITS["x"])
        found = [(y * 2 + x, near), (y * 2 + 1 - x, aside)]
        found.append(((1 - y) * 2 + x, exchange(near, BITS["y"])))
        found.append(((1 - y) * 2 + 1 - x, exchange(aside, BITS["y"])))
    elif form == 1:
        near = ring_gather(ordered_pair(own, "y", place), place)
        found = [(x, near), (1 - x, exchange(near, BITS["x"]))]
    else:
        near = ordered_pair(ordered_pair(own, "x", place), "y", place)
        found = [((z - hop) % 4, block) for hop, block in enumerate(ring_blocks(near))]
    count = near.shape[0]
    total = jnp.zeros((32,) + own.shape[1:], own.dtype)
    for at, block in found:
        total = set_block(total, block, (at * 2 + c) * count)
        total = set_block(total, exchange(block, BITS["c"]), (at * 2 + 1 - c) * count)
    return total


def take_block(value, index, parts):
    count = value.shape[0] // parts
    return lax.dynamic_slice_in_dim(value, index * count, count, 0)


def reduce_pair(value, name, place):
    sent = take_block(value, 1 - place[name], 2).astype(jnp.bfloat16)
    kept = take_block(value, place[name], 2).astype(jnp.float32)
    return kept + exchange(sent, BITS[name]).astype(jnp.float32)


def ring_reduce(value, place):
    z = place["z"]
    total = take_block(value, (z + 3) % 4, 4)
    for hop in range(1, 4):
        moved = rotate(total.astype(jnp.bfloat16)).astype(jnp.float32)
        total = moved + take_block(value, (z + 3 - hop) % 4, 4).astype(jnp.float32)
    return total


def scatter_chunk(value, form, place):
    for name in SCATTER_NAMES[form]:
        value = ring_reduce(value, place) if name == "z" else reduce_pair(value, name, place)
    return value[0]


def sum_small(value):
    for bit in (1, 2, 4, 8, 16):
        value = value + exchange(value, bit)
    return value


def pack_block(block, width):
    height, breadth = block.shape[-2:]
    lead = block.shape[:-2]
    if breadth == width:
        return block
    if width % breadth == 0 and height % (width // breadth) == 0:
        times = width // breadth
        each = height // times
        return jnp.concatenate(
            [block[..., part * each : (part + 1) * each, :] for part in range(times)], axis=-1
        )
    return block.reshape(lead + (height * breadth // width, width))


def unpack_block(block, height, breadth):
    width = block.shape[-1]
    lead = block.shape[:-2]
    if breadth == width:
        return block
    if width % breadth == 0 and height % (width // breadth) == 0:
        times = width // breadth
        return jnp.concatenate(
            [block[..., part * breadth : (part + 1) * breadth] for part in range(times)], axis=-2
        )
    return block.reshape(lead + (height, breadth))


def slot_of(names, step):
    col = step % 8
    row = step // 8
    index = {"y": row // 2, "x": row % 2, "z": col // 2, "c": col % 2}
    slot = 0
    for name in names:
        slot = slot * EXTENT[name] + index[name]
    return slot


def unpack_kernel(layout, from_ref, *to_refs):
    start = 0
    for to_ref, halves in zip(to_refs, layout):
        if halves is None:
            count = to_ref.shape[1]
            to_ref[0] = from_ref[0, start : start + count, :]
        elif halves == 1:
            count = to_ref.shape[0]
            to_ref[...] = from_ref[0, start : start + count, :]
        else:
            count = to_ref.shape[0] // 2
            breadth = to_ref.shape[1]
            to_ref[:count, :] = from_ref[0, start : start + count, :breadth]
            to_ref[count:, :] = from_ref[0, start : start + count, breadth:]
        start += count


def whole_spec(height, breadth, parts=None):
    first, last = parts or (0, 7)
    return pl.BlockSpec(
        (height, breadth),
        lambda step: (step // 8, jnp.clip(step % 8 - first, 0, last - first)),
    )


def flipped_spec(height, breadth):
    return pl.BlockSpec((height, breadth), lambda step: (step % 8, step // 8))


def halves_of(shape):
    if shape[1] == PACKED:
        return 1
    return 2 if 2 * shape[1] == PACKED else None


def unpack_chunk(total, form, pieces, chunk):
    names = GATHER_NAMES[form]
    layout = []
    specs = []
    shapes = []
    for name in chunk:
        block, flipped = pieces[name]
        height, breadth = block.shape
        halves = halves_of(block.shape)
        layout.append(halves)
        if halves is None:
            count = height * breadth // PACKED
            specs.append(pl.BlockSpec((1, count, PACKED), lambda step: (step, 0, 0)))
            shapes.append(jax.ShapeDtypeStruct((32, count, PACKED), block.dtype))
        elif flipped:
            specs.append(flipped_spec(height, breadth))
            shapes.append(jax.ShapeDtypeStruct((8 * height, 4 * breadth), block.dtype))
        else:
            specs.append(whole_spec(height, breadth))
            shapes.append(jax.ShapeDtypeStruct((4 * height, 8 * breadth), block.dtype))
    found = pl.pallas_call(
        lambda *refs: unpack_kernel(layout, *refs),
        grid=(32,),
        in_specs=[
            pl.BlockSpec((1,) + total.shape[1:], lambda step: (slot_of(names, step), 0, 0))
        ],
        out_specs=specs,
        out_shape=shapes,
        cost_estimate=pl.CostEstimate(
            flops=0, bytes_accessed=4 * total.size, transcendentals=0
        ),
        name="unpack_chunk",
    )(total)
    full = {}
    for name, value, halves in zip(chunk, found, layout):
        if halves is None:
            block, flipped = pieces[name]
            height, breadth = block.shape
            value = value.reshape(4, 8, height, breadth).transpose(1, 2, 0, 3)
            value = value.reshape(8 * height, 4 * breadth)
        full[name] = value
    return full


def pack_kernel(split, halves, refs, outs):
    step = pl.program_id(0)
    col = step % 8
    qkv_ref, out_ref, up_ref, down_ref, small_ref = refs[:5]
    top, side, deep = outs
    for part_ref, first, last in ((qkv_ref, 0, 2), (out_ref, 3, 3), (up_ref, 4, 7)):

        @pl.when(jnp.logical_and(col >= first, col <= last))
        def _():
            top[0] = part_ref[:split, :]
            rest = part_ref.shape[0] - split
            side[0, :rest, :] = part_ref[split:, :]

    rest = qkv_ref.shape[0] - split
    count = small_ref.shape[0] // 2
    breadth = small_ref.shape[1]
    side[0, rest : rest + count, :breadth] = small_ref[:count, :]
    side[0, rest : rest + count, breadth:] = small_ref[count:, :]
    if len(refs) > 5:
        side[0, rest + count :, :] = refs[5][0]
    deep[0] = down_ref[...]


def pack_chunks(grads, pieces, depth):
    wide = pieces["wide%d" % depth][0].shape
    down = pieces["down%d" % depth][0].shape
    small = "dec_wide" if depth else "embed"
    height, breadth = pieces[small][0].shape
    args = list(grads["wide%d" % depth]) + [grads["down%d" % depth], grads[small]]
    specs = [whole_spec(*wide, parts=parts) for parts in ((0, 2), (3, 3), (4, 7))]
    specs.append(flipped_spec(*down))
    specs.append((flipped_spec if pieces[small][1] else whole_spec)(height, breadth))
    side = wide[0] - SPLIT + height // 2
    if depth:
        tall, broad = pieces["dec_rows"][0].shape
        count = tall * broad // PACKED
        value = grads["dec_rows"].reshape(8, tall, 4, broad).transpose(2, 0, 1, 3)
        args.append(value.reshape(32, count, PACKED))
        specs.append(pl.BlockSpec((1, count, PACKED), lambda step: (step, 0, 0)))
        side += count
    counts = (SPLIT, side, down[0])
    number = len(args)
    return pl.pallas_call(
        lambda *refs: pack_kernel(SPLIT, 2, refs[:number], refs[number:]),
        grid=(32,),
        in_specs=specs,
        out_specs=[
            pl.BlockSpec(
                (1, count, PACKED), lambda step, names=names: (slot_of(names, step), 0, 0)
            )
            for count, names in zip(counts, SCATTER_NAMES)
        ],
        out_shape=[jax.ShapeDtypeStruct((32, count, PACKED), jnp.bfloat16) for count in counts],
        cost_estimate=pl.CostEstimate(
            flops=0, bytes_accessed=128 * sum(counts) * PACKED, transcendentals=0
        ),
        name="pack_chunks",
    )(*args)


PACKED = 768
GATHER_CHUNKS = (("wide0", "embed", "dec_rows"), ("wide1", "dec_wide"), ("down0", "down1"))
SPLIT = 144
SCATTER_NAMES_OF = {1: ("wide1", "down1", "dec_wide", "dec_rows"), 0: ("wide0", "down0", "embed")}


def gather_near(pieces, place):
    full = {}
    for form, chunk in enumerate(GATHER_CHUNKS):
        own = jnp.concatenate([pack_block(pieces[name][0], PACKED) for name in chunk], axis=0)
        total = gather_chunk(own, form, place)
        full.update(unpack_chunk(total, form, pieces, chunk))
    return full


def scatter_near(grads, pieces, depth, place):
    top, side, deep = (
        scatter_chunk(value, form, place)
        for form, value in enumerate(pack_chunks(grads, pieces, depth))
    )
    rest = pieces["wide%d" % depth][0].shape[0] - SPLIT
    small = "dec_wide" if depth else "embed"
    height, breadth = pieces[small][0].shape
    mine = {
        "wide%d" % depth: jnp.concatenate([top, side[:rest]], axis=0),
        "down%d" % depth: deep,
        small: unpack_block(side[rest : rest + height // 2], height, breadth),
    }
    if depth:
        shape = pieces["dec_rows"][0].shape
        mine["dec_rows"] = side[rest + height // 2 :].reshape(shape)
    return mine


def gather_far(pieces):
    full = {}
    for name, (block, flipped) in pieces.items():
        first, second = ("col", "row") if flipped else ("row", "col")
        across = lax.all_gather(block, second, axis=1, tiled=True)
        full[name] = lax.all_gather(across, first, axis=0, tiled=True)
    return full


def scatter_far(grads, pieces, names):
    mine = {}
    for name in names:
        if name.startswith("wide"):
            grads = dict(grads, **{name: jnp.concatenate(grads[name], axis=1)})
        row_dim = 1 if pieces[name][1] else 0
        part = lax.psum_scatter(grads[name], "row", scatter_dimension=row_dim, tiled=True)
        mine[name] = lax.psum_scatter(
            part.astype(jnp.float32), "col", scatter_dimension=1 - row_dim, tiled=True
        )
    return mine


def adam_update(master, moment, second, grad, rate, decay, count):
    moment = beta_first * moment + (1.0 - beta_first) * grad
    second = beta_second * second + (1.0 - beta_second) * grad * grad
    first_hat = moment / (1.0 - beta_first**count)
    second_hat = second / (1.0 - beta_second**count)
    master = master - rate * (first_hat / (jnp.sqrt(second_hat) + adam_epsilon) + decay * master)
    return (master, moment, second)


def shards(
    tubes,
    tube_order,
    step_count,
    embed_weight,
    embed_first,
    embed_second,
    encoder_wide_weight,
    encoder_wide_first,
    encoder_wide_second,
    encoder_down_weight,
    encoder_down_first,
    encoder_down_second,
    decoder_wide_weight,
    decoder_wide_first,
    decoder_wide_second,
    decoder_rows_weight,
    decoder_rows_first,
    decoder_rows_second,
    pixel_head_weight,
    pixel_head_first,
    pixel_head_second,
    vectors_weight,
    vectors_first,
    vectors_second,
):
    low = jnp.bfloat16
    pieces = {
        "embed": (embed_weight.astype(low).T, True),
        "dec_wide": (decoder_wide_weight.astype(low), False),
        "dec_rows": (decoder_rows_weight.astype(low).T, True),
    }
    for depth in range(L):
        pieces["wide%d" % depth] = (encoder_wide_weight[depth].astype(low), False)
        pieces["down%d" % depth] = (encoder_down_weight[depth].astype(low).T, True)
    near = (lax.axis_size("row"), lax.axis_size("col")) == (4, 8)
    place = own_place() if near else None
    weights = gather_near(pieces, place) if near else gather_far(pieces)

    def reduce_head(grad):
        return lax.psum(grad, BOTH)

    def reduce_late(grads, depth):
        if near:
            return scatter_near(grads, pieces, depth, place)
        return scatter_far(grads, pieces, SCATTER_NAMES_OF[depth])

    inverse = 1.0 / (tubes.shape[0] * lax.axis_size("row") * lax.axis_size("col") * NMASK * PIX)
    loss_local, mine, grad_head, grad_vectors = all_grads(
        weights,
        pixel_head_weight.astype(low),
        vectors_weight,
        tubes,
        tube_order,
        inverse,
        reduce_head,
        reduce_late,
    )
    small = jnp.concatenate([loss_local[None], grad_vectors])
    small = sum_small(small) if near else lax.psum(small, BOTH)
    loss = small[0]
    grads = (
        mine["embed"].T,
        jnp.stack([mine["wide%d" % depth] for depth in range(L)]),
        jnp.stack([mine["down%d" % depth].T for depth in range(L)]),
        mine["dec_wide"],
        mine["dec_rows"].T,
        grad_head,
        small[1:],
    )
    masters = (
        embed_weight,
        encoder_wide_weight,
        encoder_down_weight,
        decoder_wide_weight,
        decoder_rows_weight,
        pixel_head_weight,
        vectors_weight,
    )
    firsts = (
        embed_first,
        encoder_wide_first,
        encoder_down_first,
        decoder_wide_first,
        decoder_rows_first,
        pixel_head_first,
        vectors_first,
    )
    seconds = (
        embed_second,
        encoder_wide_second,
        encoder_down_second,
        decoder_wide_second,
        decoder_rows_second,
        pixel_head_second,
        vectors_second,
    )
    count = step_count[0].astype(jnp.float32)
    rates = (
        PIX ** (-0.5),
        D ** (-0.5),
        FF ** (-0.5),
        DD ** (-0.5),
        DFF ** (-0.5),
        DD ** (-0.5),
        0.1,
    )
    decays = (decay_factor,) * 6 + (0.0,)
    results = [loss]
    for index in range(7):
        results.extend(
            adam_update(
                masters[index],
                firsts[index],
                seconds[index],
                grads[index],
                rates[index],
                decays[index],
                count,
            )
        )
    return tuple(results)


def solution(mesh):
    placed = (
        P(("row", "col"), None, None),
        P(("row", "col"), None),
        P(),
        P("row", "col"),
        P("row", "col"),
        P("row", "col"),
        P(None, "row", "col"),
        P(None, "row", "col"),
        P(None, "row", "col"),
        P(None, "row", "col"),
        P(None, "row", "col"),
        P(None, "row", "col"),
        P("row", "col"),
        P("row", "col"),
        P("row", "col"),
        P("row", "col"),
        P("row", "col"),
        P("row", "col"),
        P(),
        P(),
        P(),
        P(),
        P(),
        P(),
    )
    return jax.shard_map(
        shards,
        mesh=mesh,
        in_specs=placed,
        out_specs=(
            P(),
            P("row", "col"),
            P("row", "col"),
            P("row", "col"),
            P(None, "row", "col"),
            P(None, "row", "col"),
            P(None, "row", "col"),
            P(None, "row", "col"),
            P(None, "row", "col"),
            P(None, "row", "col"),
            P("row", "col"),
            P("row", "col"),
            P("row", "col"),
            P("row", "col"),
            P("row", "col"),
            P("row", "col"),
            P(),
            P(),
            P(),
            P(),
            P(),
            P(),
        ),
        check_vma=False,
    )
```
